32 devices in a mesh: ctx: 4 (over z), tp: 2 (over x), dp: 4 (over y, core).
Axes of the slice: x: 2, y: 2, z: 4, core: 2. Of those that a mesh axis runs over, the one named last changes fastest.
Arguments:
- queries: bfloat16 [4, 1024, 8192], P('dp', 'ctx', 'tp'), may hold values from -80 to 80
- prompt_keys: bfloat16 [4, 1024, 1024], P('dp', 'ctx', 'tp'), may hold values from -4 to 4
- prompt_values: bfloat16 [4, 1024, 1024], P('dp', 'ctx', 'tp'), may hold values from -6 to 6
- resp_keys: bfloat16 [4, 1024, 1024], P('dp', 'ctx', 'tp'), may hold values from -4 to 4
- resp_values: bfloat16 [4, 1024, 1024], P('dp', 'ctx', 'tp'), may hold values from -6 to 6
- pattern: int32 [4, 2, 8], P('dp'), may hold values from 0 to 1, as said below
- lengths: int32 [4, 2], P('dp'), may hold values from 257 to 512, as said below
- out_weight: bfloat16 [8192, 4096], P(('tp', 'dp'), 'ctx'), may hold values from -0.0625 to 0.0625
Outputs:
- attended: bfloat16 [4, 1024, 4096], P('dp', 'ctx', 'tp')
The draws below stay inside these ranges and needn't reach their ends.
Inputs may be any that keep to these rules, and one draw needn't show every extreme that they name: pattern[g, r, 0] is 1 for every response; each response reads 4 or more blocks; in each group some response reads all 8 blocks. `lengths`: in each group some response has length 512.
All inputs are finite; a program needn't handle non-finite values.
Results may differ from the reference program's by a relative error of at most 0.013.
Values may be sent and summed in bfloat16 or wider, within the bound.
A program may use at most 192 MiB of HBM per device.

```python
import jax
import jax.numpy as jnp
from jax import lax

HQ = 64
KVH = 8
HD = 128
WOUT = 4096
BLK = 128
TOK_DEV = 256
RLEN = 512
PROMPT = 1024
RESP = 2
NBLK = 8
GROUPS = 4


def drawn_pair(key):
    key_q = jax.random.fold_in(key, 101)
    key_k = jax.random.fold_in(key, 102)
    shape_q = (GROUPS, RESP * RLEN, HQ * HD)
    shape_k = (GROUPS, PROMPT, KVH * HD)
    keys_drawn = jnp.clip(jax.random.normal(key_k, shape_k, jnp.float32), -4.0, 4.0)
    query_drawn = jnp.clip(jax.random.normal(key_q, shape_q, jnp.float32), -6.0, 6.0)
    return (query_drawn, keys_drawn)


def draw_queries(key, part):
    return drawn_pair(key)[0].astype(jnp.bfloat16)


def draw_prompt_keys(key, part):
    return drawn_pair(key)[1].astype(jnp.bfloat16)


def draw_pattern(key, part):
    key_count = jax.random.fold_in(key, 201)
    key_full = jax.random.fold_in(key, 202)
    key_rank = jax.random.fold_in(key, 203)
    counts = jax.random.randint(key_count, (GROUPS, RESP), 4, NBLK + 1)
    full_resp = jax.random.randint(key_full, (GROUPS,), 0, RESP)
    counts = jnp.where(jnp.arange(RESP, dtype=jnp.int32)[None, :] == full_resp[:, None], NBLK, counts)
    noise = jax.random.randint(key_rank, (GROUPS, RESP, NBLK - 1), 0, 1 << 20)
    noise = noise * NBLK + jnp.arange(NBLK - 1, dtype=jnp.int32)
    order = jnp.argsort(noise, axis=-1, stable=True)
    ranks = jnp.argsort(order, axis=-1, stable=True).astype(jnp.int32)
    rest = (ranks < counts[..., None] - 1).astype(jnp.int32)
    first = jnp.ones((GROUPS, RESP, 1), jnp.int32)
    return jnp.concatenate([first, rest], axis=-1)


def draw_lengths(key, part):
    key_len = jax.random.fold_in(key, 301)
    key_full = jax.random.fold_in(key, 302)
    drawn = jax.random.randint(key_len, (GROUPS, RESP), RLEN // 2 + 1, RLEN + 1)
    full_resp = jax.random.randint(key_full, (GROUPS,), 0, RESP)
    return jnp.where(jnp.arange(RESP, dtype=jnp.int32)[None, :] == full_resp[:, None], RLEN, drawn).astype(jnp.int32)


def block_scale(rng, extent, shards, least, largest):
    def one(axis_at, blocks):
        steps = jax.random.uniform(jax.random.fold_in(jax.random.fold_in(rng, 6), axis_at), (blocks,), jnp.float32, least / len(shards), largest / len(shards))
        return jnp.repeat(jnp.exp(steps), extent[axis_at] // blocks).reshape((-1,) + (1,) * (len(extent) - axis_at - 1))

    gain = one(*shards[0])
    for cut in shards[1:]:
        gain = gain * one(*cut)
    return gain


def bell_draw(rng, extent, scale, bound, cuts=(), kind=jnp.bfloat16):
    values = scale * jax.random.normal(rng, extent, jnp.float32)
    if cuts:
        values = values * block_scale(rng, extent, cuts, -0.22, 0.18)
    return jnp.clip(values, -bound, bound).astype(kind)


def setup_inputs(seed: int = 0) -> dict:
    streams_of = jax.random.split(jax.random.key(seed), 9)
    return {
        "queries": draw_queries(jax.random.fold_in(streams_of[8], 71), 0),
        "prompt_keys": draw_prompt_keys(jax.random.fold_in(streams_of[8], 71), 0),
        "prompt_values": bell_draw(streams_of[2], (GROUPS, PROMPT, KVH * HD), 1.0, 6.0, ((0, 4), (1, 4), (2, 2))),
        "resp_keys": bell_draw(streams_of[3], (GROUPS, RESP * RLEN, KVH * HD), 1.0, 4.0, ((0, 4), (1, 4), (2, 2))),
        "resp_values": bell_draw(streams_of[4], (GROUPS, RESP * RLEN, KVH * HD), 1.0, 6.0, ((0, 4), (1, 4), (2, 2))),
        "pattern": draw_pattern(jax.random.fold_in(streams_of[8], 71), 0),
        "lengths": draw_lengths(jax.random.fold_in(streams_of[8], 71), 0),
        "out_weight": bell_draw(streams_of[7], (HQ * HD, WOUT), (HQ * HD) ** -0.5, 0.0625, ((0, 8), (1, 4))),
    }


def by_response(rows):
    width = rows.shape[-1]
    return jnp.transpose(rows.reshape(2, RESP, TOK_DEV, width), (1, 0, 2, 3)).reshape(RESP, RLEN, width)


def reference(queries, prompt_keys, prompt_values, resp_keys, resp_values, pattern, lengths, out_weight):
    group = HQ // KVH
    scale = HD ** -0.5
    slots = jnp.arange(RLEN, dtype=jnp.int32)
    causal = slots[None, :] <= slots[:, None]

    def one_group(gidx):
        qall = by_response(queries[gidx]).reshape(RESP, RLEN, KVH, group, HD)
        pkeys = prompt_keys[gidx].reshape(PROMPT, KVH, HD)
        pvals = prompt_values[gidx].reshape(PROMPT, KVH, HD)
        rkeys = by_response(resp_keys[gidx]).reshape(RESP, RLEN, KVH, HD)
        rvals = by_response(resp_values[gidx]).reshape(RESP, RLEN, KVH, HD)

        def one_resp(ridx):
            blocks = pattern[gidx, ridx]
            readable = jnp.repeat(blocks, BLK) > 0

            def one_head(kidx):
                qhead = qall[ridx, :, kidx].astype(jnp.float32)
                sprompt = jnp.einsum("igd,jd->gij", qhead, pkeys[:, kidx].astype(jnp.float32)) * scale
                sown = jnp.einsum("igd,jd->gij", qhead, rkeys[ridx, :, kidx].astype(jnp.float32)) * scale
                sprompt = jnp.where(readable[None, None, :], sprompt, -jnp.inf)
                sown = jnp.where(causal[None], sown, -jnp.inf)
                top = jnp.maximum(jnp.max(sprompt, -1), jnp.max(sown, -1))
                eprompt = jnp.where(readable[None, None, :], jnp.exp(sprompt - top[..., None]), 0.0)
                eown = jnp.where(causal[None], jnp.exp(sown - top[..., None]), 0.0)
                total = jnp.sum(eprompt, -1) + jnp.sum(eown, -1)
                rprompt = eprompt.astype(jnp.bfloat16).astype(jnp.float32)
                rown = eown.astype(jnp.bfloat16).astype(jnp.float32)
                mixed = jnp.einsum("gij,jd->gid", rprompt, pvals[:, kidx].astype(jnp.float32), precision=lax.Precision.HIGHEST)
                mixed = mixed + jnp.einsum("gij,jd->gid", rown, rvals[ridx, :, kidx].astype(jnp.float32), precision=lax.Precision.HIGHEST)
                return mixed / total[..., None]

            heads = lax.map(one_head, jnp.arange(KVH, dtype=jnp.int32))
            context = jnp.transpose(heads, (2, 0, 1, 3)).reshape(RLEN, HQ * HD)
            live = slots < lengths[gidx, ridx]
            return jnp.where(live[:, None], context, 0.0).astype(jnp.bfloat16)

        context = lax.map(one_resp, jnp.arange(RESP, dtype=jnp.int32)).reshape(RESP * RLEN, HQ * HD)
        projected = jnp.dot(context, out_weight, preferred_element_type=jnp.float32).astype(jnp.bfloat16)
        projected = jnp.transpose(projected.reshape(RESP, 2, TOK_DEV, WOUT), (1, 0, 2, 3))
        return projected.reshape(RESP * RLEN, WOUT)

    return lax.map(one_group, jnp.arange(GROUPS, dtype=jnp.int32))
```

```python
import jax
import jax.numpy as jnp
from jax import lax
from jax.sharding import PartitionSpec as P

HD = 128
BLK = 128
RLEN = 512


def shifted(x, axis, by):
    devices = lax.axis_size(axis)
    pairs = [(i, i + by) for i in range(devices) if 0 <= i + by < devices]
    return lax.ppermute(x, axis, pairs)


def local(
    queries, prompt_keys, prompt_values, resp_keys, resp_values, pattern, lengths, out_weight
):
    tok = queries.shape[1]
    kv_here = prompt_keys.shape[2] // HD
    q_here = queries.shape[2] // HD
    group = q_here // kv_here
    scale = HD ** (-0.5)
    halves = RLEN // tok
    responses = lax.axis_size("ctx") // halves
    place = lax.axis_index("ctx")
    resp_id = place % responses
    half = place // responses
    positions = half * tok + jnp.arange(tok, dtype=jnp.int32)
    chosen = jnp.arange(pattern.shape[1], dtype=jnp.int32) == resp_id
    block_row = jnp.sum(jnp.where(chosen[:, None], pattern[0], 0), axis=0)
    live_len = jnp.sum(jnp.where(chosen, lengths[0], 0))
    query_heads = queries[0].reshape(tok, kv_here, group, HD)
    earlier = shifted((resp_keys, resp_values), "ctx", responses)
    own_keys = jnp.concatenate([earlier[0][0], resp_keys[0]], axis=0).reshape(2 * tok, kv_here, HD)
    own_vals = jnp.concatenate([earlier[1][0], resp_values[0]], axis=0).reshape(
        2 * tok, kv_here, HD
    )
    key_pos = (half - 1) * tok + jnp.arange(2 * tok, dtype=jnp.int32)
    allowed = (key_pos[None, :] >= 0) & (key_pos[None, :] <= positions[:, None])
    scores = (
        jnp.einsum("ikgd,jkd->kgij", query_heads, own_keys, preferred_element_type=jnp.float32)
        * scale
    )
    running = jnp.max(jnp.where(allowed, scores, -jnp.inf), axis=-1)
    probs = jnp.where(allowed, jnp.exp(scores - running[..., None]), 0.0)
    total = jnp.sum(probs, axis=-1)
    accum = jnp.einsum(
        "kgij,jkd->kgid", probs.astype(jnp.bfloat16), own_vals, preferred_element_type=jnp.float32
    )
    pieces = (
        lax.all_gather(prompt_keys, "ctx", axis=1, tiled=True),
        lax.all_gather(prompt_values, "ctx", axis=1, tiled=True),
    )
    count = pieces[0].shape[1]
    block_ids = jnp.arange(count, dtype=jnp.int32) // BLK
    onehot = block_ids[:, None] == jnp.arange(block_row.shape[0], dtype=jnp.int32)[None, :]
    readable = jnp.sum(jnp.where(onehot, block_row[None, :], 0), axis=1) > 0
    piece_keys = pieces[0][0].reshape(-1, kv_here, HD)
    piece_vals = pieces[1][0].reshape(-1, kv_here, HD)
    block_scores = (
        jnp.einsum("ikgd,jkd->kgij", query_heads, piece_keys, preferred_element_type=jnp.float32)
        * scale
    )
    mask = readable[None, None, None, :]
    new_max = jnp.maximum(running, jnp.max(jnp.where(mask, block_scores, -jnp.inf), axis=-1))
    weights = jnp.where(mask, jnp.exp(block_scores - new_max[..., None]), 0.0)
    factor = jnp.exp(running - new_max)
    new_total = total * factor + jnp.sum(weights, axis=-1)
    new_acc = accum * factor[..., None] + jnp.einsum(
        "kgij,jkd->kgid",
        weights.astype(jnp.bfloat16),
        piece_vals,
        preferred_element_type=jnp.float32,
    )
    context = new_acc / new_total[..., None]
    context = jnp.transpose(context, (2, 0, 1, 3)).reshape(tok, q_here * HD)
    context = jnp.where((positions < live_len)[:, None], context, 0.0).astype(jnp.bfloat16)
    head_rows = lax.all_gather(out_weight, "dp", axis=0, tiled=True)
    rows = lax.all_gather(context, "ctx", axis=0, tiled=True)
    columns = jnp.dot(rows, head_rows, preferred_element_type=jnp.float32).astype(jnp.bfloat16)
    partial_out = lax.all_to_all(columns, "ctx", split_axis=0, concat_axis=1, tiled=True)
    summed = lax.psum_scatter(
        partial_out, "tp", scatter_dimension=1, tiled=True
    )
    return summed[None]


def solution(mesh):
    placed = (
        P("dp", "ctx", "tp"),
        P("dp", "ctx", "tp"),
        P("dp", "ctx", "tp"),
        P("dp", "ctx", "tp"),
        P("dp", "ctx", "tp"),
        P("dp", None, None),
        P("dp", None),
        P(("tp", "dp"), "ctx"),
    )
    return jax.shard_map(
        local, mesh=mesh, in_specs=placed, out_specs=P("dp", "ctx", "tp"), check_vma=False
    )
```

```python
import jax
import jax.numpy as jnp
from jax import lax
from jax.experimental import pallas as pl
from jax.experimental.pallas import tpu as pltpu
from jax.sharding import PartitionSpec as P

HD = 128
BLK = 128
RLEN = 512


def shifted(x, axis, by):
    devices = lax.axis_size(axis)
    pairs = [(i, i + by) for i in range(devices) if 0 <= i + by < devices]
    return lax.ppermute(x, axis, pairs)


def swapped(x, axis, stride):
    return lax.ppermute(x, axis, [(i, i ^ stride) for i in range(lax.axis_size(axis))])


def attend_head(at_ref, q_ref, k_ref, v_ref, bias_ref, o_ref):
    scores = lax.dot_general(
        q_ref[...], k_ref[...], (((1,), (1,)), ((), ())), preferred_element_type=jnp.float32
    )
    scores = scores * (HD**-0.5) + bias_ref[...]
    probs = jnp.exp(scores - jnp.max(scores, axis=-1, keepdims=True))
    total = jnp.sum(probs, axis=-1, keepdims=True)
    mixed = jnp.dot(probs.astype(jnp.bfloat16), v_ref[...], preferred_element_type=jnp.float32)
    slot = lax.broadcasted_iota(jnp.int32, mixed.shape, 0)
    o_ref[...] = jnp.where(slot < at_ref[1], mixed / total, 0.0).astype(o_ref.dtype)


def attend(at, queries, keys, vals, bias, heads, group):
    tok, count = bias.shape
    return pl.pallas_call(
        attend_head,
        grid_spec=pltpu.PrefetchScalarGridSpec(
            num_scalar_prefetch=1,
            grid=(heads,),
            in_specs=[
                pl.BlockSpec((tok, HD), lambda h, at: (0, at[0] + h)),
                pl.BlockSpec((count, HD), lambda h, at: (0, (at[0] + h) // group)),
                pl.BlockSpec((count, HD), lambda h, at: (0, (at[0] + h) // group)),
                pl.BlockSpec((tok, count), lambda h, at: (0, 0)),
            ],
            out_specs=pl.BlockSpec((tok, HD), lambda h, at: (0, h)),
        ),
        out_shape=jax.ShapeDtypeStruct((tok, heads * HD), jnp.bfloat16),
        cost_estimate=pl.CostEstimate(
            flops=4 * heads * tok * count * HD,
            bytes_accessed=4 * heads * tok * HD + 4 * count * HD + 4 * tok * count,
            transcendentals=heads * tok * count,
        ),
    )(at, queries, keys, vals, bias)


def local(
    queries, prompt_keys, prompt_values, resp_keys, resp_values, pattern, lengths, out_weight
):
    tok = queries.shape[1]
    width = prompt_keys.shape[2]
    group = queries.shape[2] // width
    heads = out_weight.shape[0] // HD
    halves = RLEN // tok
    places = lax.axis_size("ctx")
    responses = places // halves
    place = lax.axis_index("ctx")
    resp_id = place % responses
    half = place // responses

    prompt = lax.all_gather(
        jnp.concatenate([prompt_keys[0], prompt_values[0]], axis=1), "ctx", axis=0, tiled=True
    )
    own = jnp.concatenate([resp_keys[0], resp_values[0]], axis=1)
    earlier = shifted(own, "ctx", responses)

    blocks = {(0, 0): out_weight}
    stride = 2
    while stride < places:
        blocks.update({(k ^ stride, j): swapped(b, "ctx", stride) for (k, j), b in blocks.items()})
        stride *= 2
    stride = lax.axis_size("dp") // 2
    while stride:
        blocks.update({(k, j ^ stride): swapped(b, "dp", stride) for (k, j), b in blocks.items()})
        stride //= 2

    chosen = jnp.arange(pattern.shape[1], dtype=jnp.int32) == resp_id
    block_row = jnp.sum(jnp.where(chosen[:, None], pattern[0], 0), axis=0)
    live_len = jnp.sum(jnp.where(chosen, lengths[0], 0))
    readable = jnp.repeat(block_row, BLK) > 0
    positions = half * tok + jnp.arange(tok, dtype=jnp.int32)
    key_pos = (half - 1) * tok + jnp.arange(2 * tok, dtype=jnp.int32)
    allowed = (key_pos[None, :] >= 0) & (key_pos[None, :] <= positions[:, None])
    allowed = jnp.concatenate(
        [jnp.broadcast_to(readable[None, :], (tok, readable.shape[0])), allowed], axis=1
    )
    bias = jnp.where(allowed, 0.0, -jnp.inf).astype(jnp.float32)
    both = jnp.concatenate([prompt, earlier, own], axis=0)
    keys, vals = both[:, :width], both[:, width:]

    sums = {}
    for j in sorted({j for _, j in blocks}, key=lambda j: (j & 1, j)):
        first = (lax.axis_index("dp") ^ j) * heads
        at = jnp.stack([first, live_len - half * tok]).astype(jnp.int32)
        context = attend(at, queries[0], keys, vals, bias, heads, group)
        rows = jnp.concatenate([context, swapped(context, "ctx", 1)], axis=0)
        for k in sorted({k for k, _ in blocks}):
            term = jnp.dot(rows, blocks[k, j], preferred_element_type=jnp.float32)
            sums[k] = sums[k] + term if k in sums else term
    mine = {}
    for k, total in sums.items():
        total = total.astype(jnp.bfloat16)
        mine[k] = total[:tok]
        mine[k ^ 1] = swapped(total[tok:], "ctx", 1)
    stacked = jnp.stack([mine[k] for k in range(places)])
    partial_out = jnp.concatenate(
        [lax.dynamic_index_in_dim(stacked, b ^ place, 0, keepdims=False) for b in range(places)],
        axis=1,
    )
    summed = lax.psum_scatter(partial_out, "tp", scatter_dimension=1, tiled=True)
    return summed[None]


def solution(mesh):
    placed = (
        P("dp", "ctx", "tp"),
        P("dp", "ctx", "tp"),
        P("dp", "ctx", "tp"),
        P("dp", "ctx", "tp"),
        P("dp", "ctx", "tp"),
        P("dp", None, None),
        P("dp", None),
        P(("tp", "dp"), "ctx"),
    )
    return jax.shard_map(
        local, mesh=mesh, in_specs=placed, out_specs=P("dp", "ctx", "tp"), check_vma=False
    )
```

```python
import jax
import jax.numpy as jnp
from jax import lax
from jax.experimental import pallas as pl
from jax.experimental.pallas import tpu as pltpu
from jax.sharding import PartitionSpec as P


HD = 128
BLK = 128
RLEN = 512


def shifted(x, axis, by):
    devices = lax.axis_size(axis)
    pairs = [(i, i + by) for i in range(devices) if 0 <= i + by < devices]
    return lax.ppermute(x, axis, pairs)


def swapped(x, axis, stride):
    return lax.ppermute(x, axis, [(i, i ^ stride) for i in range(lax.axis_size(axis))])


def spread(blocks):
    stride = lax.axis_size("dp") // 2
    while stride:
        more = {(k, j ^ stride): swapped(b, "dp", stride) for (k, j), b in blocks.items()}
        blocks = {**blocks, **more}
        stride //= 2
    return blocks


def attend_head(at_ref, q_ref, k_ref, v_ref, bias_ref, o_ref):
    scores = lax.dot_general(
        q_ref[...], k_ref[...], (((1,), (1,)), ((), ())), preferred_element_type=jnp.float32
    )
    scores = scores * (HD**-0.5) + bias_ref[...]
    probs = jnp.exp(scores - jnp.max(scores, axis=-1, keepdims=True))
    total = jnp.sum(probs, axis=-1, keepdims=True)
    mixed = jnp.dot(probs.astype(jnp.bfloat16), v_ref[...], preferred_element_type=jnp.float32)
    slot = lax.broadcasted_iota(jnp.int32, mixed.shape, 0)
    o_ref[...] = jnp.where(slot < at_ref[1], mixed / total, 0.0).astype(o_ref.dtype)


def attend(at, queries, keys, vals, bias, heads, group):
    tok, count = bias.shape
    return pl.pallas_call(
        attend_head,
        grid_spec=pltpu.PrefetchScalarGridSpec(
            num_scalar_prefetch=1,
            grid=(heads,),
            in_specs=[
                pl.BlockSpec((tok, HD), lambda h, at: (0, at[0] + h)),
                pl.BlockSpec((count, HD), lambda h, at: (0, (at[0] + h) // group)),
                pl.BlockSpec((count, HD), lambda h, at: (0, (at[0] + h) // group)),
                pl.BlockSpec((tok, count), lambda h, at: (0, 0)),
            ],
            out_specs=pl.BlockSpec((tok, HD), lambda h, at: (0, h)),
        ),
        out_shape=jax.ShapeDtypeStruct((tok, heads * HD), jnp.bfloat16),
        cost_estimate=pl.CostEstimate(
            flops=4 * heads * tok * count * HD,
            bytes_accessed=4 * heads * tok * HD + 4 * count * HD + 4 * tok * count,
            transcendentals=heads * tok * count,
        ),
    )(at, queries, keys, vals, bias)


def local(
    queries, prompt_keys, prompt_values, resp_keys, resp_values, pattern, lengths, out_weight
):
    tok = queries.shape[1]
    width = prompt_keys.shape[2]
    group = queries.shape[2] // width
    heads = out_weight.shape[0] // HD
    halves = RLEN // tok
    places = lax.axis_size("ctx")
    responses = places // halves
    place = lax.axis_index("ctx")
    resp_id = place % responses
    half = place // responses

    prompt = lax.all_gather(
        jnp.concatenate([prompt_keys[0], prompt_values[0]], axis=1), "ctx", axis=0, tiled=True
    )
    own = jnp.concatenate([resp_keys[0], resp_values[0]], axis=1)
    earlier = shifted(own, "ctx", responses)

    blocks = {(0, 0): out_weight}
    stride = 2
    while stride < places:
        blocks.update({(k ^ stride, j): swapped(b, "ctx", stride) for (k, j), b in blocks.items()})
        stride *= 2
    far = {key: b for key, b in blocks.items() if key[0]}
    blocks = spread({(0, 0): out_weight})

    chosen = jnp.arange(pattern.shape[1], dtype=jnp.int32) == resp_id
    block_row = jnp.sum(jnp.where(chosen[:, None], pattern[0], 0), axis=0)
    live_len = jnp.sum(jnp.where(chosen, lengths[0], 0))
    readable = jnp.repeat(block_row, BLK) > 0
    positions = half * tok + jnp.arange(tok, dtype=jnp.int32)
    key_pos = (half - 1) * tok + jnp.arange(2 * tok, dtype=jnp.int32)
    allowed = (key_pos[None, :] >= 0) & (key_pos[None, :] <= positions[:, None])
    allowed = jnp.concatenate(
        [jnp.broadcast_to(readable[None, :], (tok, readable.shape[0])), allowed], axis=1
    )
    bias = jnp.where(allowed, 0.0, -jnp.inf).astype(jnp.float32)
    both = jnp.concatenate([prompt, earlier, own], axis=0)
    keys, vals = both[:, :width], both[:, width:]

    sums = {}
    gathered = []
    for j in sorted({j for _, j in blocks}, key=lambda j: (j & 1, j)):
        first = (lax.axis_index("dp") ^ j) * heads
        at = jnp.stack([first, live_len - half * tok]).astype(jnp.int32)
        context = attend(at, queries[0], keys, vals, bias, heads, group)
        gathered.append((j, context, swapped(context, "ctx", 1)))
        if len(gathered) == 2:
            far = dict(zip(far, lax.optimization_barrier((*far.values(), context))))
            blocks.update(spread(far))
    for j, context, paired in gathered:
        rows = jnp.concatenate([context, paired], axis=0)
        for k in sorted({k for k, _ in blocks}):
            term = jnp.dot(rows, blocks[k, j], preferred_element_type=jnp.float32)
            sums[k] = sums[k] + term if k in sums else term
    mine = {}
    for k, total in sums.items():
        total = total.astype(jnp.bfloat16)
        mine[k] = total[:tok]
        mine[k ^ 1] = swapped(total[tok:], "ctx", 1)
    stacked = jnp.stack([mine[k] for k in range(places)])
    partial_out = jnp.concatenate(
        [lax.dynamic_index_in_dim(stacked, b ^ place, 0, keepdims=False) for b in range(places)],
        axis=1,
    )
    summed = lax.psum_scatter(partial_out, "tp", scatter_dimension=1, tiled=True)
    return summed[None]


def solution(mesh):
    placed = (
        P("dp", "ctx", "tp"),
        P("dp", "ctx", "tp"),
        P("dp", "ctx", "tp"),
        P("dp", "ctx", "tp"),
        P("dp", "ctx", "tp"),
        P("dp", None, None),
        P("dp", None),
        P(("tp", "dp"), "ctx"),
    )
    return jax.shard_map(
        local, mesh=mesh, in_specs=placed, out_specs=P("dp", "ctx", "tp"), check_vma=False
    )
```
